32 devices in a mesh: hid: 8 (over y, x, core), ep: 4 (over z).
Axes of the slice: x: 2, y: 2, z: 4, core: 2. Of those that a mesh axis runs over, the one named last changes fastest.
Arguments:
- tokens: bfloat16 [2048, 2048], P('ep', 'hid'), may hold values from -6 to 6
- expert_ids: int32 [2048, 6], P('ep'), may hold values from 0 to 15, all different within a row; in each aligned block of 512 rows (0 to 511, 512 to 1023, ...) at most 256 rows name the same one
- gate_weights: float32 [2048, 6], P('ep'), may hold values from 0.1 to 1
- w_gate_up: bfloat16 [4, 5632, 2, 2048], P('ep', 'hid'), may hold values from -0.125 to 0.125
- w_down: bfloat16 [4, 5632, 2048], P('ep', 'hid'), may hold values from -0.21875 to 0.21875
Outputs:
- mixed: bfloat16 [2048, 2048], P('ep', 'hid')
The draws below stay inside these ranges and needn't reach their ends.
Inputs may be any that keep to these rules, and one draw needn't show every extreme that they name: `expert_ids`: the 6 ids of a row differ. Among the 512 rows of one index of ep (aligned blocks of rows), no expert is named by more than 256 rows.
All inputs are finite; a program needn't handle non-finite values.
Results may differ from the reference program's by a relative error of at most 0.0064.
Values may be sent and summed in bfloat16 or wider, within the bound.
A program may use at most 64 MiB of HBM per device.

```python
import math
import jax
import jax.numpy as jnp
import numpy as np
from jax import lax

D = 2048
FF = 1408
TOPK = 6
EXP_DEV = 4
TOK_EP = 512
EXPERTS = 16
SHARDS = 2
CAP = 256
TOKENS = 2048
N_EP = 4


def raised(entries, key, source, target, blocks, factor):
    def block_of(dim):
        return (jnp.arange(entries.shape[dim]) // (entries.shape[dim] // blocks)).reshape((-1,) + (1,) * (entries.ndim - 1 - dim))

    first = jax.random.permutation(key, blocks)[block_of(target)]
    other_side = (block_of(target) + blocks // 2) % blocks
    return jnp.where((block_of(source) == first) | (block_of(source) == other_side), factor * entries, entries)


def steps_of(key, dims, cuts, smallest, largest):
    factor_of, own = 1.0, jax.random.fold_in(key, 6)
    for axis_at, shards_of in cuts:
        draws = jnp.exp(jax.random.uniform(jax.random.fold_in(own, axis_at), (shards_of,), jnp.float32, smallest / len(cuts), largest / len(cuts)))
        factor_of = factor_of * jnp.repeat(draws, dims[axis_at] // shards_of).reshape([-1 if axis == axis_at else 1 for axis in range(len(dims))])
    return factor_of


def assign_block(key, own, number, rows, count, top, bound, lean):
    order = jax.random.permutation(key, count)
    heavy_load, common = portions_of(count, rows * top, bound, lean, True), portions_of(count, rows * top, bound, lean, False)
    places = jnp.arange(count)

    def named(sizes, offset_by):
        used = int((sizes > 0).sum())
        fixed = max(1, used // 4)
        moved = fixed + (places - fixed + offset_by * (used - fixed)) % max(1, count - fixed)
        return jnp.zeros((count,), jnp.int32).at[order[jnp.where(places < fixed, places, moved)]].set(jnp.asarray(sizes, jnp.int32))

    sizes = jnp.where(number % 4 == 0, named(heavy_load, number // 4), named(common, number - number // 4 - 1))
    mixed = jax.random.permutation(jax.random.fold_in(own, 3), count)
    source_of, receiver = mixed[0:count // 2 * 2:2], mixed[1:count // 2 * 2:2]
    margin = jnp.minimum(sizes[source_of] - 1, bound - sizes[receiver]) // 2
    margin = jnp.where((source_of == order[0]) | (receiver == order[0]) | (sizes[receiver] == 0), 0, jnp.maximum(margin, 0))
    moved = jax.random.randint(jax.random.fold_in(own, 4), (count // 2,), 0, 1 << 20) % (margin + 1)
    sizes = sizes.at[source_of].add(-moved).at[receiver].add(moved)
    labels = jnp.searchsorted(jnp.cumsum(sizes), jnp.arange(rows * top), side="right").astype(jnp.int32)
    table = labels.reshape(top, rows).T
    table = table[jax.random.permutation(jax.random.fold_in(own, 1), rows)]
    offset_by = jax.random.randint(jax.random.fold_in(own, 2), (rows, 1), 0, top)
    return jnp.take_along_axis(table, (jnp.arange(top)[None, :] + offset_by) % top, axis=1)


def portions_of(amount, total, limit, slope, full):
    portions = [(1 << 20) // math.isqrt(standing ** slope) + 1 for standing in range(1, amount + 1)]
    largest = limit if full else min(limit, max(-(-total // amount), total * portions[0] // sum(portions)))
    least = 1 if total - largest >= amount - 1 else 0
    given, surplus = [largest] + [least] * (amount - 1), total - largest - least * (amount - 1)
    while surplus > 0:
        free = [i for i in range(1, amount) if given[i] < largest] or [i for i in range(1, amount) if given[i] < limit]
        pool, left = sum([portions[i] for i in free]), surplus
        for i in free:
            extra = min(limit - given[i], max(1, left * portions[i] // pool), surplus)
            given[i] = given[i] + extra
            surplus = surplus - extra
    return np.array(given)


def bell_draw(key, dims, deviation, bound, shards=(), kind=jnp.bfloat16):
    drawn = deviation * jax.random.normal(key, dims, jnp.float32)
    if shards:
        drawn = drawn * steps_of(key, dims, shards, -0.22, 0.18)
    return jnp.clip(drawn, -bound, bound).astype(kind)


def heavy_noise(key, dims, scale, limit, split, heavy, kind=jnp.bfloat16):
    drawn = scale * jax.random.normal(key, dims, jnp.float32)
    if split:
        drawn = drawn * steps_of(key, dims, split, -0.22, 0.18)
    return jnp.clip(raised(drawn, jax.random.fold_in(key, 3), *heavy), -limit, limit).astype(kind)


def setup_inputs(seed: int = 0) -> dict:
    seeds = jax.random.split(jax.random.key(seed), 6)
    tokens = bell_draw(seeds[0], (TOKENS, D), 1.0, 6.0, ((0, 4), (1, 8)))
    expert_ids_keys = jax.random.split(jax.random.fold_in(seeds[1], 1), TOKENS // TOK_EP)
    expert_ids_turns = jax.random.permutation(jax.random.fold_in(seeds[1], 3), TOKENS // TOK_EP)
    expert_ids = jax.vmap(lambda own, number: assign_block(jax.random.fold_in(seeds[1], 2), own, number, TOK_EP, EXPERTS, TOPK, CAP, 2))(expert_ids_keys, expert_ids_turns).reshape((TOKENS, TOPK))
    gate_weights = jnp.clip(0.1 + 0.9 * jax.random.uniform(seeds[2], (TOKENS, TOPK), jnp.float32) ** steps_of(seeds[2], (TOKENS, TOPK), ((0, 4),), -0.2, 0.2), 0.1, 1.0)
    w_gate_up = bell_draw(seeds[3], (N_EP, EXP_DEV * FF, 2, D), D ** -0.5, 0.125, ((0, 4), (1, 8)))
    w_down = heavy_noise(seeds[4], (N_EP, EXP_DEV * FF, D), FF ** -0.5, 0.21875, ((0, 4), (1, 8)), (1, 2, 8, 2.0))
    return {"tokens": tokens, "expert_ids": expert_ids, "gate_weights": gate_weights, "w_gate_up": w_gate_up, "w_down": w_down}


def slot_numbers(ids, count):
    flat = ids.reshape(-1)
    onehot = (flat[:, None] == jnp.arange(count, dtype=jnp.int32)[None, :]).astype(jnp.int32)
    before = jnp.cumsum(onehot, axis=0) - onehot
    return jnp.sum(before * onehot, axis=1).astype(jnp.int32).reshape(ids.shape)


def reference(tokens, expert_ids, gate_weights, w_gate_up, w_down):
    blocks = expert_ids.reshape(N_EP, TOK_EP, TOPK)
    slot = jax.vmap(lambda b: slot_numbers(b, EXPERTS))(blocks).reshape(TOKENS, TOPK)
    token_index = jnp.broadcast_to(jnp.arange(TOKENS, dtype=jnp.int32)[:, None], (TOKENS, TOPK))
    block_index = (token_index // TOK_EP).astype(jnp.int32)
    position = (block_index * CAP + slot).astype(jnp.int32)
    table = jnp.full((EXPERTS, N_EP * CAP), TOKENS, dtype=jnp.int32).at[expert_ids, position].set(token_index)
    padded = jnp.concatenate([tokens, jnp.zeros((1, D), jnp.bfloat16)], axis=0)
    all_up = w_gate_up.reshape(EXPERTS, FF, 2, D)
    all_down = w_down.reshape(EXPERTS, FF, D)

    def per_expert(packed):
        rows_index, weights_up, weights_down = packed
        rows = padded[rows_index]
        gate = jnp.dot(rows, weights_up[:, 0, :].T, preferred_element_type=jnp.float32)
        upper = jnp.dot(rows, weights_up[:, 1, :].T, preferred_element_type=jnp.float32)
        hidden = (jax.nn.silu(gate) * upper).astype(jnp.bfloat16)
        count = rows.shape[0]
        grouped = hidden.reshape(count, SHARDS, FF // SHARDS).astype(jnp.float32)
        down = weights_down.reshape(SHARDS, FF // SHARDS, D).astype(jnp.float32)
        parts = jnp.einsum("rjf,jfd->rjd", grouped, down)
        parts = lax.optimization_barrier(parts.astype(jnp.bfloat16)).astype(jnp.float32)
        return jnp.sum(parts, axis=1).astype(jnp.bfloat16)

    results = lax.map(per_expert, (table, all_up, all_down))
    flat = results.reshape(EXPERTS * N_EP * CAP, D)
    picked = flat[(expert_ids * (N_EP * CAP) + position).astype(jnp.int32)]
    mixed = jnp.sum(picked.astype(jnp.float32) * gate_weights[:, :, None], axis=1)
    return mixed.astype(jnp.bfloat16)
```

```python
import functools

import jax
import jax.numpy as jnp
from jax import lax
from jax.experimental import pallas as pl
from jax.experimental.pallas import tpu as pltpu
from jax.sharding import PartitionSpec as P

EXP_DEV = 4
MESH = pl.DeviceIdType.MESH


def partner_at(me, step, count):
    if count & (count - 1):
        return lax.rem(me + step, count)
    found, bit = 0, 1
    while bit < count:
        found = found + (((me // bit) % 2 + (step // bit) % 2) % 2) * bit
        bit *= 2
    return found


def layer_kernel(
    groups, hid_count, capacity,
    tok_ref, ids_ref, gates_ref, up_hbm, down_hbm, out_ref,
    w_pair, w_gate, w_up, w_down, meta, meta_in, x_all, r_send, rows,
    p_buf, p_in, y_send, y_in, z_send, z_in, own,
    load_sem, tok_ss, tok_rs, meta_ss, meta_rs, row_ss, row_rs, keep_sem,
    fwd_ss, fwd_rs, part_ss, part_rs, y_ss, y_rs, z_ss, z_rs,
):
    shards = hid_count // EXP_DEV
    tok_rows, width = tok_ref.shape
    experts = EXP_DEV * groups
    ep = lax.axis_index("ep")
    hid = lax.axis_index("hid")
    mine = hid // shards
    core = hid % shards

    def place(h):
        return pl.ds(pl.multiple_of(h * width, 128), width)

    def at(e, c):
        return e * shards + c

    def z_dev(g):
        return {"ep": g, "hid": hid}

    def h_dev(h):
        return {"ep": ep, "hid": h}

    def remote(src, dst, ss, rs, dev):
        return pltpu.make_async_remote_copy(
            src_ref=src, dst_ref=dst, send_sem=ss, recv_sem=rs, device_id=dev, device_id_type=MESH
        )

    load_up = pltpu.make_async_copy(up_hbm, w_pair, load_sem.at[0])
    load_down = pltpu.make_async_copy(down_hbm, w_down, load_sem.at[1])
    load_up.start()
    load_down.start()

    barrier = pltpu.get_barrier_semaphore()
    peers = [z_dev(partner_at(ep, s, groups)) for s in range(1, groups)]
    peers += [h_dev(at((mine + k) % EXP_DEV, core)) for k in range(1, EXP_DEV)]
    peers += [h_dev(at(mine, (core + j) % shards)) for j in range(1, shards)]
    for dev in peers:
        pl.semaphore_signal(barrier, inc=1, device_id=dev, device_id_type=MESH)

    eid = lax.broadcasted_iota(jnp.int32, (experts, tok_rows), 0)
    hit = jnp.zeros((experts, tok_rows), jnp.float32)
    gate = jnp.zeros((experts, tok_rows), jnp.float32)
    for k in range(ids_ref.shape[0]):
        same = ids_ref[k : k + 1, :] == eid
        hit = hit + jnp.where(same, 1.0, 0.0)
        gate = gate + jnp.where(same, gates_ref[k : k + 1, :], 0.0)
    earlier = lax.broadcasted_iota(jnp.int32, (tok_rows, tok_rows), 0) < lax.broadcasted_iota(
        jnp.int32, (tok_rows, tok_rows), 1
    )
    before = jnp.dot(
        hit.astype(jnp.bfloat16),
        jnp.where(earlier, 1.0, 0.0).astype(jnp.bfloat16),
        preferred_element_type=jnp.float32,
    )
    slot = jnp.where(hit > 0.5, before, -1.0)
    for g in range(groups):
        meta[g, 0:EXP_DEV] = slot[g * EXP_DEV : (g + 1) * EXP_DEV]
        meta[g, EXP_DEV : 2 * EXP_DEV] = gate[g * EXP_DEV : (g + 1) * EXP_DEV]

    pl.semaphore_wait(barrier, len(peers))

    def tok_copy(s):
        g = partner_at(ep, s, groups)
        return remote(tok_ref, x_all.at[ep], tok_ss.at[s], tok_rs.at[s], z_dev(g))

    def meta_copy(s):
        g = partner_at(ep, s, groups)
        return remote(meta.at[g], meta_in.at[ep], meta_ss.at[s], meta_rs.at[s], z_dev(g))

    for s in range(1, groups):
        meta_copy(s).start()
        tok_copy(s).start()
    x_all[ep] = tok_ref[...]
    meta_in[ep] = meta[ep]

    load_up.wait()
    load_down.wait()
    step_rows = 16

    def split(i, carry):
        r = pl.ds(pl.multiple_of(i * step_rows, step_rows), step_rows)
        w_gate[r, :] = w_pair[r, 0, :]
        w_up[r, :] = w_pair[r, 1, :]
        return carry

    lax.fori_loop(0, w_gate.shape[0] // step_rows, split, 0)

    def row_copy(b, k):
        e = (mine + k) % EXP_DEV
        return remote(r_send.at[b, e], rows.at[b, :, place(hid)], row_ss.at[b, k], row_rs.at[b, k], h_dev(at(e, core)))

    def keep_copy(b):
        return pltpu.make_async_copy(r_send.at[b, mine], rows.at[b, :, place(hid)], keep_sem.at[b])

    def fwd_copy(b, k, j):
        other = h_dev(at(mine, (core + j) % shards))
        h = at((mine + EXP_DEV - k) % EXP_DEV, core)
        src = r_send.at[b, mine] if k == 0 else rows.at[b, :, place(h)]
        return remote(src, rows.at[b, :, place(h)], fwd_ss.at[b, k, j], fwd_rs.at[b, k, j], other)

    def part_copy(b, j):
        c = (core + j) % shards
        return remote(p_buf.at[b, c], p_in.at[b, j], part_ss.at[b, j], part_rs.at[b, j], h_dev(at(mine, c)))

    def y_copy(b, k):
        e = (mine + k) % EXP_DEV
        return remote(y_send.at[b, e], y_in.at[b, mine], y_ss.at[b, k], y_rs.at[b, k], h_dev(at(e, core)))

    def z_copy(s):
        g = partner_at(ep, s, groups)
        return remote(z_send.at[s], z_in.at[s], z_ss.at[s], z_rs.at[s], z_dev(g))

    slot_id = lax.broadcasted_iota(jnp.int32, (capacity, tok_rows), 0).astype(jnp.float32)

    def stage_rows(s):
        b = partner_at(ep, s, groups)

        @pl.when(s > 0)
        def _():
            meta_copy(s).wait_recv()
            tok_copy(s).wait_recv()

        x = x_all[b]
        for e in range(EXP_DEV):
            pick = jnp.where(meta_in[b, e : e + 1, :] == slot_id, 1.0, 0.0).astype(jnp.bfloat16)
            r_send[b, e] = jnp.dot(pick, x, preferred_element_type=jnp.float32).astype(jnp.bfloat16)
        for k in (2, 1, 3):
            row_copy(b, k).start()
        keep_copy(b).start()
        for j in range(1, shards):
            fwd_copy(b, 0, j).start()

    def stage_forward(s):
        b = partner_at(ep, s, groups)
        for k in (1, 3, 2):
            row_from(b, k).wait_recv()
            for j in range(1, shards):
                fwd_copy(b, k, j).start()

    def stage_experts(s):
        b = partner_at(ep, s, groups)
        keep_copy(b).wait()
        for k in range(EXP_DEV):
            for j in range(1, shards):
                fwd_copy(b, k, j).wait_recv()
        x = rows[b]
        nt = (((1,), (1,)), ((), ()))
        gate = lax.dot_general(x, w_gate[...], nt, preferred_element_type=jnp.float32)
        up = lax.dot_general(x, w_up[...], nt, preferred_element_type=jnp.float32)
        hidden = (gate / (1.0 + jnp.exp(-gate)) * up).astype(jnp.bfloat16)
        for c in range(shards):
            for e in range(EXP_DEV):
                cols = slice(at(e, c) * width, (at(e, c) + 1) * width)
                p_buf[b, c, e] = jnp.dot(
                    hidden, w_down[:, cols], preferred_element_type=jnp.float32
                ).astype(jnp.bfloat16)
        for j in range(1, shards):
            part_copy(b, j).start()

    def stage_sum(s):
        b = partner_at(ep, s, groups)
        for j in range(1, shards):
            part_copy(b, j).wait_recv()
        for e in range(EXP_DEV):
            y = p_buf[b, core, e].astype(jnp.float32)
            for j in range(1, shards):
                y = y + p_in[b, j, e].astype(jnp.float32)
            y_send[b, e] = y.astype(jnp.bfloat16)
        for k in (2, 1, 3):
            y_copy(b, k).start()
        y_in[b, mine] = y_send[b, mine]

    def stage_mix(s):
        b = partner_at(ep, s, groups)
        for k in (1, 3, 2):
            y_from(b, k).wait_recv()
        total = jnp.zeros((tok_rows, width), jnp.float32)
        for e in range(EXP_DEV):
            spread = jnp.where(
                meta_in[b, e : e + 1, :] == slot_id, meta_in[b, EXP_DEV + e : EXP_DEV + e + 1, :], 0.0
            ).astype(jnp.bfloat16)
            total = total + lax.dot_general(
                spread, y_in[b, e], (((0,), (0,)), ((), ())), preferred_element_type=jnp.float32
            )

        @pl.when(s == 0)
        def _():
            own[...] = total

        @pl.when(s > 0)
        def _():
            z_send[s] = total.astype(jnp.bfloat16)
            z_copy(s).start()

    def y_from(b, k):
        e = (mine + EXP_DEV - k) % EXP_DEV
        return remote(y_send.at[b, e], y_in.at[b, e], y_ss.at[b, k], y_rs.at[b, k], h_dev(at(e, core)))

    def row_from(b, k):
        e = (mine + EXP_DEV - k) % EXP_DEV
        return remote(r_send.at[b, e], rows.at[b, :, place(at(e, core))], row_ss.at[b, k], row_rs.at[b, k], h_dev(at(e, core)))

    def tick(t, carry):
        for lag, stage in ((0, stage_rows), (1, stage_forward), (3, stage_sum), (4, stage_mix), (2, stage_experts)):
            s = t - lag

            @pl.when((s >= 0) & (s < groups))
            def _():
                stage(s)

        return carry

    lax.fori_loop(0, groups + 4, tick, 0)

    total = own[...]
    for s in range(1, groups):
        z_copy(s).wait_recv()
        total = total + z_in[s].astype(jnp.float32)
    out_ref[...] = total.astype(out_ref.dtype)

    for s in range(1, groups):
        meta_copy(s).wait_send()
        tok_copy(s).wait_send()
        z_copy(s).wait_send()

    def drain(b, carry):
        for k in range(1, EXP_DEV):
            row_copy(b, k).wait_send()
            y_copy(b, k).wait_send()
        for j in range(1, shards):
            part_copy(b, j).wait_send()
            for k in range(EXP_DEV):
                fwd_copy(b, k, j).wait_send()
        return carry

    lax.fori_loop(0, groups, drain, 0)


def fused_layer(tokens, expert_ids, gate_weights, w_gate_up, w_down):
    groups = lax.axis_size("ep")
    hid_count = lax.axis_size("hid")
    shards = hid_count // EXP_DEV
    tok_rows, width = tokens.shape
    topk = expert_ids.shape[1]
    capacity = tok_rows * topk * 4 // (3 * EXP_DEV * groups)
    units, _, depth = w_gate_up.shape[1:]
    bf, dma = jnp.bfloat16, pltpu.SemaphoreType.DMA
    vmem = pl.BlockSpec(memory_space=pltpu.VMEM)
    hbm = pl.BlockSpec(memory_space=pl.ANY)
    block = (capacity, width)
    return pl.pallas_call(
        functools.partial(layer_kernel, groups, hid_count, capacity),
        out_shape=jax.ShapeDtypeStruct((tok_rows, width), bf),
        in_specs=[vmem, vmem, vmem, hbm, hbm],
        out_specs=vmem,
        scratch_shapes=[
            pltpu.VMEM((units, 2, depth), bf),
            pltpu.VMEM((units, depth), bf),
            pltpu.VMEM((units, depth), bf),
            pltpu.VMEM((units, depth), bf),
            pltpu.VMEM((groups, 2 * EXP_DEV, tok_rows), jnp.float32),
            pltpu.VMEM((groups, 2 * EXP_DEV, tok_rows), jnp.float32),
            pltpu.VMEM((groups, tok_rows, width), bf),
            pltpu.VMEM((groups, EXP_DEV) + block, bf),
            pltpu.VMEM((groups, capacity, depth), bf),
            pltpu.VMEM((groups, shards, EXP_DEV) + block, bf),
            pltpu.VMEM((groups, shards, EXP_DEV) + block, bf),
            pltpu.VMEM((groups, EXP_DEV) + block, bf),
            pltpu.VMEM((groups, EXP_DEV) + block, bf),
            pltpu.VMEM((groups, tok_rows, width), bf),
            pltpu.VMEM((groups, tok_rows, width), bf),
            pltpu.VMEM((tok_rows, width), jnp.float32),
            dma((2,)),
            dma((groups,)),
            dma((groups,)),
            dma((groups,)),
            dma((groups,)),
            dma((groups, EXP_DEV)),
            dma((groups, EXP_DEV)),
            dma((groups,)),
            dma((groups, EXP_DEV, shards)),
            dma((groups, EXP_DEV, shards)),
            dma((groups, shards)),
            dma((groups, shards)),
            dma((groups, EXP_DEV)),
            dma((groups, EXP_DEV)),
            dma((groups,)),
            dma((groups,)),
        ],
        compiler_params=pltpu.CompilerParams(
            collective_id=0, has_side_effects=True, vmem_limit_bytes=60 * 1024 * 1024
        ),
    )(tokens, expert_ids.T, gate_weights.T, w_gate_up[0], w_down[0])


def slot_numbers(ids, count):
    flat = ids.reshape(-1)
    onehot = (flat[:, None] == jnp.arange(count, dtype=jnp.int32)[None, :]).astype(jnp.int32)
    before = jnp.cumsum(onehot, axis=0) - onehot
    return jnp.sum(before * onehot, axis=1).reshape(ids.shape)


def on_device(tokens, expert_ids, gate_weights, w_gate_up, w_down):
    groups = lax.axis_size("ep")
    hid_count = lax.axis_size("hid")
    shards = hid_count // EXP_DEV
    experts = EXP_DEV * groups
    tok_rows = tokens.shape[0]
    width_local = tokens.shape[1]
    topk = expert_ids.shape[1]
    capacity = tok_rows * topk * 4 // (3 * experts)
    rows_per = groups * capacity
    slot = slot_numbers(expert_ids, experts)
    token_index = jnp.broadcast_to(jnp.arange(tok_rows, dtype=jnp.int32)[:, None], expert_ids.shape)
    table = (
        jnp.full((experts, capacity), tok_rows, dtype=jnp.int32)
        .at[expert_ids, slot]
        .set(token_index)
    )
    padded = jnp.concatenate([tokens, jnp.zeros((1, width_local), tokens.dtype)], axis=0)
    placed = padded[table].reshape(groups, EXP_DEV, capacity, width_local)
    arrived = lax.all_to_all(placed, "ep", split_axis=0, concat_axis=2, tiled=True)[0]
    repeated = jnp.repeat(arrived, shards, axis=0)
    outgoing = jnp.transpose(repeated, (1, 0, 2)).reshape(rows_per, hid_count * width_local)
    full_rows = lax.all_to_all(outgoing, "hid", split_axis=1, concat_axis=1, tiled=True)
    gate_up = jnp.einsum("rd,fgd->gfr", full_rows, w_gate_up[0], preferred_element_type=jnp.float32)
    hidden = (jax.nn.silu(gate_up[0]) * gate_up[1]).astype(jnp.bfloat16)
    partial_value = jnp.einsum("fr,fd->rd", hidden, w_down[0], preferred_element_type=jnp.float32)
    rounded = partial_value.astype(jnp.bfloat16)
    homed = lax.all_to_all(
        rounded.reshape(1, groups, capacity, rounded.shape[1]),
        "ep",
        split_axis=1,
        concat_axis=0,
        tiled=True,
    )
    moved = lax.all_to_all(homed, "hid", split_axis=3, concat_axis=0, tiled=True)
    grouped = moved.reshape(EXP_DEV, shards, groups, capacity, width_local).astype(jnp.float32)
    summed = jnp.sum(grouped, axis=1).astype(jnp.bfloat16)
    back = jnp.transpose(summed, (1, 0, 2, 3))
    flat = back.reshape(experts * capacity, width_local)
    picked = flat[expert_ids * capacity + slot]
    mixed = jnp.sum(picked.astype(jnp.float32) * gate_weights[:, :, None], axis=1)
    return mixed.astype(jnp.bfloat16)


def solution(mesh):
    def layer(tokens, *rest):
        fits = tokens.shape[1] % 128 == 0
        return (fused_layer if fits else on_device)(tokens, *rest)

    return jax.shard_map(
        layer,
        mesh=mesh,
        in_specs=(
            P("ep", "hid"),
            P("ep", None),
            P("ep", None),
            P("ep", "hid", None, None),
            P("ep", "hid", None),
        ),
        out_specs=P("ep", "hid"),
        check_vma=False,
    )
```

```python
import functools

import jax
import jax.numpy as jnp
from jax import lax
from jax.experimental import pallas as pl
from jax.experimental.pallas import tpu as pltpu
from jax.sharding import PartitionSpec as P

EXP_DEV = 4
MESH = pl.DeviceIdType.MESH


def block_at(me, step, count):
    if step == 0:
        return me
    far = 1 - 2 * ((2 * me) // count)
    short = me * ((1 + far) // 2) + (count - 1 - me) * ((1 - far) // 2)
    half = (step + 1) // 2
    both = me + far * (half if step % 2 else -half)
    return jnp.where(step <= 2 * short, both, me + far * (step - short))


def layer_kernel(
    groups, hid_count, capacity,
    tok_ref, ids_ref, gates_ref, up_hbm, down_hbm, out_ref,
    w_pair, w_gate, w_up, w_down, meta, meta_in, x_all, r_send, rows,
    p_buf, p_in, y_send, y_in, z_send, z_in, own,
    load_sem, tok_ss, tok_rs, meta_ss, meta_rs, row_ss, row_rs, keep_sem,
    fwd_ss, fwd_rs, part_ss, part_rs, y_ss, y_rs, z_ss, z_rs,
):
    shards = hid_count // EXP_DEV
    tok_rows, width = tok_ref.shape
    experts = EXP_DEV * groups
    ep = lax.axis_index("ep")
    hid = lax.axis_index("hid")
    mine = hid // shards
    core = hid % shards

    def place(h):
        return pl.ds(pl.multiple_of(h * width, 128), width)

    def at(e, c):
        return e * shards + c

    def z_dev(g):
        return {"ep": g, "hid": hid}

    def h_dev(h):
        return {"ep": ep, "hid": h}

    def remote(src, dst, ss, rs, dev):
        return pltpu.make_async_remote_copy(
            src_ref=src, dst_ref=dst, send_sem=ss, recv_sem=rs, device_id=dev, device_id_type=MESH
        )

    load_up = pltpu.make_async_copy(up_hbm, w_pair, load_sem.at[0])
    load_down = pltpu.make_async_copy(down_hbm, w_down, load_sem.at[1])
    load_up.start()
    load_down.start()

    barrier = pltpu.get_barrier_semaphore()
    order = [block_at(ep, s, groups) for s in range(groups)]
    peers = [z_dev(g) for g in order[1:]]
    peers += [h_dev(at((mine + k) % EXP_DEV, core)) for k in range(1, EXP_DEV)]
    peers += [h_dev(at(mine, (core + j) % shards)) for j in range(1, shards)]
    for dev in peers:
        pl.semaphore_signal(barrier, inc=1, device_id=dev, device_id_type=MESH)

    eid = lax.broadcasted_iota(jnp.int32, (experts, tok_rows), 0)
    hit = jnp.zeros((experts, tok_rows), jnp.float32)
    gate = jnp.zeros((experts, tok_rows), jnp.float32)
    for k in range(ids_ref.shape[0]):
        same = ids_ref[k : k + 1, :] == eid
        hit = hit + jnp.where(same, 1.0, 0.0)
        gate = gate + jnp.where(same, gates_ref[k : k + 1, :], 0.0)
    earlier = lax.broadcasted_iota(jnp.int32, (tok_rows, tok_rows), 0) < lax.broadcasted_iota(
        jnp.int32, (tok_rows, tok_rows), 1
    )
    before = jnp.dot(
        hit.astype(jnp.bfloat16),
        jnp.where(earlier, 1.0, 0.0).astype(jnp.bfloat16),
        preferred_element_type=jnp.float32,
    )
    slot = jnp.where(hit > 0.5, before, -1.0)
    for g in range(groups):
        meta[g, 0:EXP_DEV] = slot[g * EXP_DEV : (g + 1) * EXP_DEV]
        meta[g, EXP_DEV : 2 * EXP_DEV] = gate[g * EXP_DEV : (g + 1) * EXP_DEV]

    pl.semaphore_wait(barrier, len(peers))

    def tok_copy(b, towards):
        src = x_all.at[b]
        return remote(src, x_all.at[b], tok_ss.at[b, (towards + 1) // 2], tok_rs.at[b], z_dev(ep + towards))

    def own_tok_copy(towards):
        return remote(tok_ref, x_all.at[ep], tok_ss.at[ep, (towards + 1) // 2], tok_rs.at[ep], z_dev(ep + towards))

    def meta_copy(s):
        g = order[s]
        return remote(meta.at[g], meta_in.at[ep], meta_ss.at[s], meta_rs.at[ep], z_dev(g))

    def meta_from(s):
        g = order[s]
        return remote(meta.at[g], meta_in.at[g], meta_ss.at[s], meta_rs.at[g], z_dev(g))

    def when_up(fn):
        pl.when(ep < groups - 1)(fn)

    def when_down(fn):
        pl.when(ep > 0)(fn)

    for s in range(1, groups):
        meta_copy(s).start()
    when_up(lambda: own_tok_copy(1).start())
    when_down(lambda: own_tok_copy(-1).start())
    x_all[ep] = tok_ref[...]
    meta_in[ep] = meta[ep]

    step_rows = 16
    pieces = w_gate.shape[0] // step_rows

    def split(i, carry):
        r = pl.ds(pl.multiple_of(i * step_rows, step_rows), step_rows)
        w_gate[r, :] = w_pair[r, 0, :]
        w_up[r, :] = w_pair[r, 1, :]
        return carry

    def row_copy(b, k):
        e = (mine + k) % EXP_DEV
        return remote(r_send.at[b, e], rows.at[b, :, place(hid)], row_ss.at[b, k], row_rs.at[b, k], h_dev(at(e, core)))

    def keep_copy(b):
        return pltpu.make_async_copy(r_send.at[b, mine], rows.at[b, :, place(hid)], keep_sem.at[b])

    def fwd_copy(b, k, j):
        other = h_dev(at(mine, (core + j) % shards))
        h = at((mine + EXP_DEV - k) % EXP_DEV, core)
        src = r_send.at[b, mine] if k == 0 else rows.at[b, :, place(h)]
        return remote(src, rows.at[b, :, place(h)], fwd_ss.at[b, k, j], fwd_rs.at[b, k, j], other)

    def part_copy(b, j):
        c = (core + j) % shards
        return remote(p_buf.at[b, c], p_in.at[b, j], part_ss.at[b, j], part_rs.at[b, j], h_dev(at(mine, c)))

    def y_copy(b, k):
        e = (mine + k) % EXP_DEV
        return remote(y_send.at[b, e], y_in.at[b, mine], y_ss.at[b, k], y_rs.at[b, k], h_dev(at(e, core)))

    def z_copy(s):
        g = order[s]
        return remote(z_send.at[s], z_in.at[ep], z_ss.at[s], z_rs.at[ep], z_dev(g))

    def z_from(s):
        g = order[s]
        return remote(z_send.at[s], z_in.at[g], z_ss.at[s], z_rs.at[g], z_dev(g))

    slot_id = lax.broadcasted_iota(jnp.int32, (capacity, tok_rows), 0).astype(jnp.float32)

    def stage_rows(s):
        b = order[s]

        if s > 0:
            meta_from(s).wait_recv()
            tok_copy(b, 1).wait_recv()
            pl.when((b < ep) & (ep < groups - 1))(lambda: tok_copy(b, 1).start())
            pl.when((b > ep) & (ep > 0))(lambda: tok_copy(b, -1).start())

        x = x_all[b]
        for e in range(EXP_DEV):
            pick = jnp.where(meta_in[b, e : e + 1, :] == slot_id, 1.0, 0.0).astype(jnp.bfloat16)
            r_send[b, e] = jnp.dot(pick, x, preferred_element_type=jnp.float32).astype(jnp.bfloat16)
        for k in (2, 1, 3):
            row_copy(b, k).start()
        keep_copy(b).start()
        for j in range(1, shards):
            fwd_copy(b, 0, j).start()

    def stage_forward(s):
        b = order[s]
        for k in (1, 3, 2):
            row_from(b, k).wait_recv()
            for j in range(1, shards):
                fwd_copy(b, k, j).start()

    def stage_experts(s):
        b = order[s]
        keep_copy(b).wait()
        for k in range(EXP_DEV):
            for j in range(1, shards):
                fwd_copy(b, k, j).wait_recv()
        x = rows[b]
        nt = (((1,), (1,)), ((), ()))
        gate = lax.dot_general(x, w_gate[...], nt, preferred_element_type=jnp.float32)
        up = lax.dot_general(x, w_up[...], nt, preferred_element_type=jnp.float32)
        hidden = (gate / (1.0 + jnp.exp(-gate)) * up).astype(jnp.bfloat16)
        for c in range(shards):
            for e in range(EXP_DEV):
                cols = slice(at(e, c) * width, (at(e, c) + 1) * width)
                p_buf[b, c, e] = jnp.dot(
                    hidden, w_down[:, cols], preferred_element_type=jnp.float32
                ).astype(jnp.bfloat16)
        for j in range(1, shards):
            part_copy(b, j).start()

    def stage_sum(s):
        b = order[s]
        for j in range(1, shards):
            part_copy(b, j).wait_recv()
        for e in range(EXP_DEV):
            y = p_buf[b, core, e].astype(jnp.float32)
            for j in range(1, shards):
                y = y + p_in[b, j, e].astype(jnp.float32)
            y_send[b, e] = y.astype(jnp.bfloat16)
        for k in (2, 1, 3):
            y_copy(b, k).start()
        y_in[b, mine] = y_send[b, mine]

    def stage_mix(s):
        b = order[s]
        for k in (1, 3, 2):
            y_from(b, k).wait_recv()
        total = jnp.zeros((tok_rows, width), jnp.float32)
        for e in range(EXP_DEV):
            spread = jnp.where(
                meta_in[b, e : e + 1, :] == slot_id, meta_in[b, EXP_DEV + e : EXP_DEV + e + 1, :], 0.0
            ).astype(jnp.bfloat16)
            total = total + lax.dot_general(
                spread, y_in[b, e], (((0,), (0,)), ((), ())), preferred_element_type=jnp.float32
            )

        if s == 0:
            own[...] = total
        else:
            z_send[s] = total.astype(jnp.bfloat16)
            z_copy(s).start()

    def y_from(b, k):
        e = (mine + EXP_DEV - k) % EXP_DEV
        return remote(y_send.at[b, e], y_in.at[b, e], y_ss.at[b, k], y_rs.at[b, k], h_dev(at(e, core)))

    def row_from(b, k):
        e = (mine + EXP_DEV - k) % EXP_DEV
        return remote(r_send.at[b, e], rows.at[b, :, place(at(e, core))], row_ss.at[b, k], row_rs.at[b, k], h_dev(at(e, core)))

    load_up.wait()
    load_down.wait()
    late = list(range(1, groups)) + [0]
    for t in range(groups + 5):
        if t < groups:
            stage_rows(t)
        if t < 2:
            lax.fori_loop(t * (pieces // 2), pieces if t else pieces // 2, split, 0)
        if 1 <= t <= groups:
            stage_forward(t - 1)
        for lag, stage in ((3, stage_sum), (4, stage_mix), (2, stage_experts)):
            if 0 <= t - lag < groups:
                stage(late[t - lag])

    total = own[...]
    for s in range(1, groups):
        z_from(s).wait_recv()
        total = total + z_in[order[s]].astype(jnp.float32)
    out_ref[...] = total.astype(out_ref.dtype)

    when_up(lambda: own_tok_copy(1).wait_send())
    when_down(lambda: own_tok_copy(-1).wait_send())
    for s in range(1, groups):
        b = order[s]
        meta_copy(s).wait_send()
        pl.when((b < ep) & (ep < groups - 1))(lambda: tok_copy(b, 1).wait_send())
        pl.when((b > ep) & (ep > 0))(lambda: tok_copy(b, -1).wait_send())
        z_copy(s).wait_send()

    def drain(b, carry):
        for k in range(1, EXP_DEV):
            row_copy(b, k).wait_send()
            y_copy(b, k).wait_send()
        for j in range(1, shards):
            part_copy(b, j).wait_send()
            for k in range(EXP_DEV):
                fwd_copy(b, k, j).wait_send()
        return carry

    lax.fori_loop(0, groups, drain, 0)


def fused_layer(tokens, expert_ids, gate_weights, w_gate_up, w_down):
    groups = lax.axis_size("ep")
    hid_count = lax.axis_size("hid")
    shards = hid_count // EXP_DEV
    tok_rows, width = tokens.shape
    topk = expert_ids.shape[1]
    capacity = tok_rows * topk * 4 // (3 * EXP_DEV * groups)
    units, _, depth = w_gate_up.shape[1:]
    bf, dma = jnp.bfloat16, pltpu.SemaphoreType.DMA
    vmem = pl.BlockSpec(memory_space=pltpu.VMEM)
    hbm = pl.BlockSpec(memory_space=pl.ANY)
    block = (capacity, width)
    return pl.pallas_call(
        functools.partial(layer_kernel, groups, hid_count, capacity),
        out_shape=jax.ShapeDtypeStruct((tok_rows, width), bf),
        in_specs=[vmem, vmem, vmem, hbm, hbm],
        out_specs=vmem,
        scratch_shapes=[
            pltpu.VMEM((units, 2, depth), bf),
            pltpu.VMEM((units, depth), bf),
            pltpu.VMEM((units, depth), bf),
            pltpu.VMEM((units, depth), bf),
            pltpu.VMEM((groups, 2 * EXP_DEV, tok_rows), jnp.float32),
            pltpu.VMEM((groups, 2 * EXP_DEV, tok_rows), jnp.float32),
            pltpu.VMEM((groups, tok_rows, width), bf),
            pltpu.VMEM((groups, EXP_DEV) + block, bf),
            pltpu.VMEM((groups, capacity, depth), bf),
            pltpu.VMEM((groups, shards, EXP_DEV) + block, bf),
            pltpu.VMEM((groups, shards, EXP_DEV) + block, bf),
            pltpu.VMEM((groups, EXP_DEV) + block, bf),
            pltpu.VMEM((groups, EXP_DEV) + block, bf),
            pltpu.VMEM((groups, tok_rows, width), bf),
            pltpu.VMEM((groups, tok_rows, width), bf),
            pltpu.VMEM((tok_rows, width), jnp.float32),
            dma((2,)),
            dma((groups, 2)),
            dma((groups,)),
            dma((groups,)),
            dma((groups,)),
            dma((groups, EXP_DEV)),
            dma((groups, EXP_DEV)),
            dma((groups,)),
            dma((groups, EXP_DEV, shards)),
            dma((groups, EXP_DEV, shards)),
            dma((groups, shards)),
            dma((groups, shards)),
            dma((groups, EXP_DEV)),
            dma((groups, EXP_DEV)),
            dma((groups,)),
            dma((groups,)),
        ],
        compiler_params=pltpu.CompilerParams(
            collective_id=0, has_side_effects=True, vmem_limit_bytes=60 * 1024 * 1024
        ),
    )(tokens, expert_ids.T, gate_weights.T, w_gate_up[0], w_down[0])


def slot_numbers(ids, count):
    flat = ids.reshape(-1)
    onehot = (flat[:, None] == jnp.arange(count, dtype=jnp.int32)[None, :]).astype(jnp.int32)
    before = jnp.cumsum(onehot, axis=0) - onehot
    return jnp.sum(before * onehot, axis=1).reshape(ids.shape)


def on_device(tokens, expert_ids, gate_weights, w_gate_up, w_down):
    groups = lax.axis_size("ep")
    hid_count = lax.axis_size("hid")
    shards = hid_count // EXP_DEV
    experts = EXP_DEV * groups
    tok_rows = tokens.shape[0]
    width_local = tokens.shape[1]
    topk = expert_ids.shape[1]
    capacity = tok_rows * topk * 4 // (3 * experts)
    rows_per = groups * capacity
    slot = slot_numbers(expert_ids, experts)
    token_index = jnp.broadcast_to(jnp.arange(tok_rows, dtype=jnp.int32)[:, None], expert_ids.shape)
    table = (
        jnp.full((experts, capacity), tok_rows, dtype=jnp.int32)
        .at[expert_ids, slot]
        .set(token_index)
    )
    padded = jnp.concatenate([tokens, jnp.zeros((1, width_local), tokens.dtype)], axis=0)
    placed = padded[table].reshape(groups, EXP_DEV, capacity, width_local)
    arrived = lax.all_to_all(placed, "ep", split_axis=0, concat_axis=2, tiled=True)[0]
    repeated = jnp.repeat(arrived, shards, axis=0)
    outgoing = jnp.transpose(repeated, (1, 0, 2)).reshape(rows_per, hid_count * width_local)
    full_rows = lax.all_to_all(outgoing, "hid", split_axis=1, concat_axis=1, tiled=True)
    gate_up = jnp.einsum("rd,fgd->gfr", full_rows, w_gate_up[0], preferred_element_type=jnp.float32)
    hidden = (jax.nn.silu(gate_up[0]) * gate_up[1]).astype(jnp.bfloat16)
    partial_value = jnp.einsum("fr,fd->rd", hidden, w_down[0], preferred_element_type=jnp.float32)
    rounded = partial_value.astype(jnp.bfloat16)
    homed = lax.all_to_all(
        rounded.reshape(1, groups, capacity, rounded.shape[1]),
        "ep",
        split_axis=1,
        concat_axis=0,
        tiled=True,
    )
    moved = lax.all_to_all(homed, "hid", split_axis=3, concat_axis=0, tiled=True)
    grouped = moved.reshape(EXP_DEV, shards, groups, capacity, width_local).astype(jnp.float32)
    summed = jnp.sum(grouped, axis=1).astype(jnp.bfloat16)
    back = jnp.transpose(summed, (1, 0, 2, 3))
    flat = back.reshape(experts * capacity, width_local)
    picked = flat[expert_ids * capacity + slot]
    mixed = jnp.sum(picked.astype(jnp.float32) * gate_weights[:, :, None], axis=1)
    return mixed.astype(jnp.bfloat16)


def solution(mesh):
    def layer(tokens, *rest):
        fits = tokens.shape[1] % 128 == 0
        return (fused_layer if fits else on_device)(tokens, *rest)

    return jax.shard_map(
        layer,
        mesh=mesh,
        in_specs=(
            P("ep", "hid"),
            P("ep", None),
            P("ep", None),
            P("ep", "hid", None, None),
            P("ep", "hid", None),
        ),
        out_specs=P("ep", "hid"),
        check_vma=False,
    )
```

```python
import functools

import jax
import jax.numpy as jnp
from jax import lax
from jax.experimental import pallas as pl
from jax.experimental.pallas import tpu as pltpu
from jax.sharding import PartitionSpec as P

EXP_DEV = 4
MESH = pl.DeviceIdType.MESH


def block_at(me, step, count):
    if step == 0:
        return me
    far = 1 - 2 * ((2 * me) // count)
    short = me * ((1 + far) // 2) + (count - 1 - me) * ((1 - far) // 2)
    half = (step + 1) // 2
    both = me + far * (half if step % 2 else -half)
    return jnp.where(step <= 2 * short, both, me + far * (step - short))


def layer_kernel(
    groups, hid_count, capacity,
    tok_ref, ids_ref, gates_ref, up_hbm, down_hbm, out_ref,
    w_pair, w_gate, w_up, w_down, meta, meta_in, x_all, r_send, rows,
    p_buf, p_in, y_send, y_in, z_send, z_in, own,
    load_sem, tok_ss, tok_rs, meta_ss, meta_rs, row_ss, row_rs, keep_sem,
    fwd_ss, fwd_rs, part_ss, part_rs, y_ss, y_rs, z_ss, z_rs,
):
    shards = hid_count // EXP_DEV
    tok_rows, width = tok_ref.shape
    experts = EXP_DEV * groups
    ep = lax.axis_index("ep")
    hid = lax.axis_index("hid")
    mine = hid // shards
    core = hid % shards

    def place(h):
        return pl.ds(pl.multiple_of(h * width, 128), width)

    def at(e, c):
        return e * shards + c

    def z_dev(g):
        return {"ep": g, "hid": hid}

    def h_dev(h):
        return {"ep": ep, "hid": h}

    def remote(src, dst, ss, rs, dev):
        return pltpu.make_async_remote_copy(
            src_ref=src, dst_ref=dst, send_sem=ss, recv_sem=rs, device_id=dev, device_id_type=MESH
        )

    load_up = pltpu.make_async_copy(up_hbm, w_pair, load_sem.at[0])
    load_down = pltpu.make_async_copy(down_hbm, w_down, load_sem.at[1])
    load_up.start()
    load_down.start()

    barrier = pltpu.get_barrier_semaphore()
    order = [block_at(ep, s, groups) for s in range(groups)]
    peers = [z_dev(g) for g in order[1:]]
    peers += [h_dev(at((mine + k) % EXP_DEV, core)) for k in range(1, EXP_DEV)]
    peers += [h_dev(at(mine, (core + j) % shards)) for j in range(1, shards)]
    for dev in peers:
        pl.semaphore_signal(barrier, inc=1, device_id=dev, device_id_type=MESH)

    eid = lax.broadcasted_iota(jnp.int32, (experts, tok_rows), 0)
    hit = jnp.zeros((experts, tok_rows), jnp.float32)
    gate = jnp.zeros((experts, tok_rows), jnp.float32)
    for k in range(ids_ref.shape[0]):
        same = ids_ref[k : k + 1, :] == eid
        hit = hit + jnp.where(same, 1.0, 0.0)
        gate = gate + jnp.where(same, gates_ref[k : k + 1, :], 0.0)
    earlier = lax.broadcasted_iota(jnp.int32, (tok_rows, tok_rows), 0) < lax.broadcasted_iota(
        jnp.int32, (tok_rows, tok_rows), 1
    )
    before = jnp.dot(
        hit.astype(jnp.bfloat16),
        jnp.where(earlier, 1.0, 0.0).astype(jnp.bfloat16),
        preferred_element_type=jnp.float32,
    )
    slot = jnp.where(hit > 0.5, before, -1.0)
    for g in range(groups):
        meta[g, 0:EXP_DEV] = slot[g * EXP_DEV : (g + 1) * EXP_DEV]
        meta[g, EXP_DEV : 2 * EXP_DEV] = gate[g * EXP_DEV : (g + 1) * EXP_DEV]

    pl.semaphore_wait(barrier, len(peers))

    def tok_copy(b, towards):
        src = x_all.at[b]
        return remote(src, x_all.at[b], tok_ss.at[b, (towards + 1) // 2], tok_rs.at[b], z_dev(ep + towards))

    def own_tok_copy(towards):
        return remote(tok_ref, x_all.at[ep], tok_ss.at[ep, (towards + 1) // 2], tok_rs.at[ep], z_dev(ep + towards))

    def meta_copy(s):
        g = order[s]
        return remote(meta.at[g], meta_in.at[ep], meta_ss.at[s], meta_rs.at[ep], z_dev(g))

    def meta_from(s):
        g = order[s]
        return remote(meta.at[g], meta_in.at[g], meta_ss.at[s], meta_rs.at[g], z_dev(g))

    def when_up(fn):
        pl.when(ep < groups - 1)(fn)

    def when_down(fn):
        pl.when(ep > 0)(fn)

    for s in range(1, groups):
        meta_copy(s).start()
    when_up(lambda: own_tok_copy(1).start())
    when_down(lambda: own_tok_copy(-1).start())
    x_all[ep] = tok_ref[...]
    meta_in[ep] = meta[ep]

    step_rows = 16
    pieces = w_gate.shape[0] // step_rows

    def split(i, carry):
        r = pl.ds(pl.multiple_of(i * step_rows, step_rows), step_rows)
        w_gate[r, :] = w_pair[r, 0, :]
        w_up[r, :] = w_pair[r, 1, :]
        return carry

    def row_copy(b, k):
        e = (mine + k) % EXP_DEV
        return remote(r_send.at[b, e], rows.at[b, :, place(hid)], row_ss.at[b, k], row_rs.at[b, k], h_dev(at(e, core)))

    def keep_copy(b):
        return pltpu.make_async_copy(r_send.at[b, mine], rows.at[b, :, place(hid)], keep_sem.at[b])

    def fwd_copy(b, k, j):
        other = h_dev(at(mine, (core + j) % shards))
        h = at((mine + EXP_DEV - k) % EXP_DEV, core)
        src = r_send.at[b, mine] if k == 0 else rows.at[b, :, place(h)]
        return remote(src, rows.at[b, :, place(h)], fwd_ss.at[b, k, j], fwd_rs.at[b, k, j], other)

    def part_copy(b, j):
        c = (core + j) % shards
        return remote(p_buf.at[b, c], p_in.at[b, j], part_ss.at[b, j], part_rs.at[b, j], h_dev(at(mine, c)))

    def y_copy(b, k):
        e = (mine + k) % EXP_DEV
        return remote(y_send.at[b, e], y_in.at[b, mine], y_ss.at[b, k], y_rs.at[b, k], h_dev(at(e, core)))

    def z_copy(s):
        g = order[s]
        return remote(z_send.at[s], z_in.at[ep], z_ss.at[s], z_rs.at[ep], z_dev(g))

    def z_from(s):
        g = order[s]
        return remote(z_send.at[s], z_in.at[g], z_ss.at[s], z_rs.at[g], z_dev(g))

    slot_id = lax.broadcasted_iota(jnp.int32, (capacity, tok_rows), 0).astype(jnp.float32)

    def stage_rows(s):
        b = order[s]

        if s > 0:
            meta_from(s).wait_recv()
            tok_copy(b, 1).wait_recv()
            pl.when((b < ep) & (ep < groups - 1))(lambda: tok_copy(b, 1).start())
            pl.when((b > ep) & (ep > 0))(lambda: tok_copy(b, -1).start())

        x = x_all[b]
        for e in range(EXP_DEV):
            pick = jnp.where(meta_in[b, e : e + 1, :] == slot_id, 1.0, 0.0).astype(jnp.bfloat16)
            r_send[b, e] = jnp.dot(pick, x, preferred_element_type=jnp.float32).astype(jnp.bfloat16)
        for k in (2, 1, 3):
            row_copy(b, k).start()
        keep_copy(b).start()
        for j in range(1, shards):
            fwd_copy(b, 0, j).start()

    def stage_forward(s):
        b = order[s]
        for k in (1, 3, 2):
            row_from(b, k).wait_recv()
            for j in range(1, shards):
                fwd_copy(b, k, j).start()

    def stage_experts(s):
        b = order[s]
        keep_copy(b).wait()
        for k in range(EXP_DEV):
            for j in range(1, shards):
                fwd_copy(b, k, j).wait_recv()
        x = rows[b]
        nt = (((1,), (1,)), ((), ()))
        gate = lax.dot_general(x, w_gate[...], nt, preferred_element_type=jnp.float32)
        up = lax.dot_general(x, w_up[...], nt, preferred_element_type=jnp.float32)
        hidden = (gate / (1.0 + jnp.exp(-gate)) * up).astype(jnp.bfloat16)
        for c in range(shards):
            for e in range(EXP_DEV):
                cols = slice(at(e, c) * width, (at(e, c) + 1) * width)
                p_buf[b, c, e] = jnp.dot(
                    hidden, w_down[:, cols], preferred_element_type=jnp.float32
                ).astype(jnp.bfloat16)
        for j in range(1, shards):
            part_copy(b, j).start()

    def stage_sum(s):
        b = order[s]
        for j in range(1, shards):
            part_copy(b, j).wait_recv()
        for e in range(EXP_DEV):
            y = p_buf[b, core, e].astype(jnp.float32)
            for j in range(1, shards):
                y = y + p_in[b, j, e].astype(jnp.float32)
            y_send[b, e] = y.astype(jnp.bfloat16)
        for k in (2, 1, 3):
            y_copy(b, k).start()
        y_in[b, mine] = y_send[b, mine]

    def stage_mix(s):
        b = order[s]
        for k in (1, 3, 2):
            y_from(b, k).wait_recv()
        total = jnp.zeros((tok_rows, width), jnp.float32)
        for e in range(EXP_DEV):
            spread = jnp.where(
                meta_in[b, e : e + 1, :] == slot_id, meta_in[b, EXP_DEV + e : EXP_DEV + e + 1, :], 0.0
            ).astype(jnp.bfloat16)
            total = total + lax.dot_general(
                spread, y_in[b, e], (((0,), (0,)), ((), ())), preferred_element_type=jnp.float32
            )

        if s == 0:
            own[...] = total
        else:
            z_send[s] = total.astype(jnp.bfloat16)
            z_copy(s).start()

    def y_from(b, k):
        e = (mine + EXP_DEV - k) % EXP_DEV
        return remote(y_send.at[b, e], y_in.at[b, e], y_ss.at[b, k], y_rs.at[b, k], h_dev(at(e, core)))

    def row_from(b, k):
        e = (mine + EXP_DEV - k) % EXP_DEV
        return remote(r_send.at[b, e], rows.at[b, :, place(at(e, core))], row_ss.at[b, k], row_rs.at[b, k], h_dev(at(e, core)))

    load_up.wait()
    load_down.wait()
    def stage_split(part):
        lax.fori_loop(part * (pieces // 2), pieces if part else pieces // 2, split, 0)

    last = groups - 1
    stage_rows(0)
    stage_split(0)
    stage_rows(1)
    stage_split(1)
    stage_forward(0)
    for s in range(2, groups):
        stage_rows(s)
        stage_forward(s - 1)
        stage_experts(s - 1)
        stage_sum(s - 1)
        if s > 2:
            stage_mix(s - 2)
    stage_forward(last)
    stage_experts(last)
    stage_sum(last)
    stage_experts(0)
    stage_mix(last - 1)
    stage_sum(0)
    stage_mix(last)
    stage_mix(0)

    total = own[...]
    for s in range(1, groups):
        z_from(s).wait_recv()
        total = total + z_in[order[s]].astype(jnp.float32)
    out_ref[...] = total.astype(out_ref.dtype)

    when_up(lambda: own_tok_copy(1).wait_send())
    when_down(lambda: own_tok_copy(-1).wait_send())
    for s in range(1, groups):
        b = order[s]
        meta_copy(s).wait_send()
        pl.when((b < ep) & (ep < groups - 1))(lambda: tok_copy(b, 1).wait_send())
        pl.when((b > ep) & (ep > 0))(lambda: tok_copy(b, -1).wait_send())
        z_copy(s).wait_send()

    def drain(b, carry):
        for k in range(1, EXP_DEV):
            row_copy(b, k).wait_send()
            y_copy(b, k).wait_send()
        for j in range(1, shards):
            part_copy(b, j).wait_send()
            for k in range(EXP_DEV):
                fwd_copy(b, k, j).wait_send()
        return carry

    lax.fori_loop(0, groups, drain, 0)


def fused_layer(tokens, expert_ids, gate_weights, w_gate_up, w_down):
    groups = lax.axis_size("ep")
    hid_count = lax.axis_size("hid")
    shards = hid_count // EXP_DEV
    tok_rows, width = tokens.shape
    topk = expert_ids.shape[1]
    capacity = tok_rows * topk * 4 // (3 * EXP_DEV * groups)
    units, _, depth = w_gate_up.shape[1:]
    bf, dma = jnp.bfloat16, pltpu.SemaphoreType.DMA
    vmem = pl.BlockSpec(memory_space=pltpu.VMEM)
    hbm = pl.BlockSpec(memory_space=pl.ANY)
    block = (capacity, width)
    return pl.pallas_call(
        functools.partial(layer_kernel, groups, hid_count, capacity),
        out_shape=jax.ShapeDtypeStruct((tok_rows, width), bf),
        in_specs=[vmem, vmem, vmem, hbm, hbm],
        out_specs=vmem,
        scratch_shapes=[
            pltpu.VMEM((units, 2, depth), bf),
            pltpu.VMEM((units, depth), bf),
            pltpu.VMEM((units, depth), bf),
            pltpu.VMEM((units, depth), bf),
            pltpu.VMEM((groups, 2 * EXP_DEV, tok_rows), jnp.float32),
            pltpu.VMEM((groups, 2 * EXP_DEV, tok_rows), jnp.float32),
            pltpu.VMEM((groups, tok_rows, width), bf),
            pltpu.VMEM((groups, EXP_DEV) + block, bf),
            pltpu.VMEM((groups, capacity, depth), bf),
            pltpu.VMEM((groups, shards, EXP_DEV) + block, bf),
            pltpu.VMEM((groups, shards, EXP_DEV) + block, bf),
            pltpu.VMEM((groups, EXP_DEV) + block, bf),
            pltpu.VMEM((groups, EXP_DEV) + block, bf),
            pltpu.VMEM((groups, tok_rows, width), bf),
            pltpu.VMEM((groups, tok_rows, width), bf),
            pltpu.VMEM((tok_rows, width), jnp.float32),
            dma((2,)),
            dma((groups, 2)),
            dma((groups,)),
            dma((groups,)),
            dma((groups,)),
            dma((groups, EXP_DEV)),
            dma((groups, EXP_DEV)),
            dma((groups,)),
            dma((groups, EXP_DEV, shards)),
            dma((groups, EXP_DEV, shards)),
            dma((groups, shards)),
            dma((groups, shards)),
            dma((groups, EXP_DEV)),
            dma((groups, EXP_DEV)),
            dma((groups,)),
            dma((groups,)),
        ],
        compiler_params=pltpu.CompilerParams(
            collective_id=0, has_side_effects=True, vmem_limit_bytes=60 * 1024 * 1024
        ),
    )(tokens, expert_ids.T, gate_weights.T, w_gate_up[0], w_down[0])


def slot_numbers(ids, count):
    flat = ids.reshape(-1)
    onehot = (flat[:, None] == jnp.arange(count, dtype=jnp.int32)[None, :]).astype(jnp.int32)
    before = jnp.cumsum(onehot, axis=0) - onehot
    return jnp.sum(before * onehot, axis=1).reshape(ids.shape)


def on_device(tokens, expert_ids, gate_weights, w_gate_up, w_down):
    groups = lax.axis_size("ep")
    hid_count = lax.axis_size("hid")
    shards = hid_count // EXP_DEV
    experts = EXP_DEV * groups
    tok_rows = tokens.shape[0]
    width_local = tokens.shape[1]
    topk = expert_ids.shape[1]
    capacity = tok_rows * topk * 4 // (3 * experts)
    rows_per = groups * capacity
    slot = slot_numbers(expert_ids, experts)
    token_index = jnp.broadcast_to(jnp.arange(tok_rows, dtype=jnp.int32)[:, None], expert_ids.shape)
    table = (
        jnp.full((experts, capacity), tok_rows, dtype=jnp.int32)
        .at[expert_ids, slot]
        .set(token_index)
    )
    padded = jnp.concatenate([tokens, jnp.zeros((1, width_local), tokens.dtype)], axis=0)
    placed = padded[table].reshape(groups, EXP_DEV, capacity, width_local)
    arrived = lax.all_to_all(placed, "ep", split_axis=0, concat_axis=2, tiled=True)[0]
    repeated = jnp.repeat(arrived, shards, axis=0)
    outgoing = jnp.transpose(repeated, (1, 0, 2)).reshape(rows_per, hid_count * width_local)
    full_rows = lax.all_to_all(outgoing, "hid", split_axis=1, concat_axis=1, tiled=True)
    gate_up = jnp.einsum("rd,fgd->gfr", full_rows, w_gate_up[0], preferred_element_type=jnp.float32)
    hidden = (jax.nn.silu(gate_up[0]) * gate_up[1]).astype(jnp.bfloat16)
    partial_value = jnp.einsum("fr,fd->rd", hidden, w_down[0], preferred_element_type=jnp.float32)
    rounded = partial_value.astype(jnp.bfloat16)
    homed = lax.all_to_all(
        rounded.reshape(1, groups, capacity, rounded.shape[1]),
        "ep",
        split_axis=1,
        concat_axis=0,
        tiled=True,
    )
    moved = lax.all_to_all(homed, "hid", split_axis=3, concat_axis=0, tiled=True)
    grouped = moved.reshape(EXP_DEV, shards, groups, capacity, width_local).astype(jnp.float32)
    summed = jnp.sum(grouped, axis=1).astype(jnp.bfloat16)
    back = jnp.transpose(summed, (1, 0, 2, 3))
    flat = back.reshape(experts * capacity, width_local)
    picked = flat[expert_ids * capacity + slot]
    mixed = jnp.sum(picked.astype(jnp.float32) * gate_weights[:, :, None], axis=1)
    return mixed.astype(jnp.bfloat16)


def solution(mesh):
    def layer(tokens, *rest):
        fits = tokens.shape[1] % 128 == 0 and mesh.shape["ep"] > 2
        return (fused_layer if fits else on_device)(tokens, *rest)

    return jax.shard_map(
        layer,
        mesh=mesh,
        in_specs=(
            P("ep", "hid"),
            P("ep", None),
            P("ep", None),
            P("ep", "hid", None, None),
            P("ep", "hid", None),
        ),
        out_specs=P("ep", "hid"),
        check_vma=False,
    )
```
